32 devices in a mesh: row: 8 (over z, x), col: 4 (over y, core).
Axes of the slice: x: 2, y: 2, z: 4, core: 2. Of those that a mesh axis runs over, the one named last changes fastest.
Arguments:
- object_slices: float32 [2, 4, 2048, 1024], P(None, None, 'row', 'col'), may hold values from -1 to 1
- positions: int32 [8, 4, 2, 2], P('row', 'col'), may hold values from 0 to 128
- intensities: float32 [8, 4, 2, 256, 256], P('row', 'col'), may hold values from 0 to 0.8
- probe: float32 [2, 256, 256], replicated, may hold values from -6 to 6
- propagator: float32 [256, 256], replicated, may hold values from -3.140625 to 3.140625
Outputs:
- gradient: float32 [2, 4, 2048, 1024], P(None, None, 'row', 'col')
- updated: float32 [2, 4, 2048, 1024], P(None, None, 'row', 'col')
The draws below stay inside these ranges and needn't reach their ends.
Inputs may be any that keep to these rules, and one draw needn't show every extreme that they name: `positions`: each probe window lies inside its tile widened by 64 pixels on every side.
All inputs are finite; a program needn't handle non-finite values.
Results may differ from the reference program's by a relative error of at most 0.0003.
Values sent between devices are 32-bit elements; how exact they have to be, the bound alone decides.
A program may use at most 128 MiB of HBM per device.

```python
import jax
import jax.numpy as jnp
from jax import lax

CORE = 256
HALO = 64
W = 256
SLICES = 4
PROBES = 2
NY = 2048
NX = 1024
N_ROW = 8
N_COL = 4


def plant(entries, rng, smallest, high):
    shape = entries.shape
    place = [jax.random.randint(jax.random.fold_in(rng, axis), (), 0, shape[axis]) for axis in range(len(shape))]
    entries = entries.at[tuple(place)].set(smallest)
    longest = shape.index(max(shape))
    place[longest] = (place[longest] + 1) % shape[longest]
    return entries.at[tuple(place)].set(high)


def block_scale(stream_key, dims, split, low, top_value):
    gain, own = 1.0, jax.random.fold_in(stream_key, 6)
    for axis_at, shards_of in split:
        heights = jnp.exp(jax.random.uniform(jax.random.fold_in(own, axis_at), (shards_of,), jnp.float32, low / len(split), top_value / len(split)))
        gain = gain * jnp.repeat(heights, dims[axis_at] // shards_of).reshape([-1 if axis == axis_at else 1 for axis in range(len(dims))])
    return gain


def bell_draw(rng, extent, scale, limit, held_as=jnp.bfloat16):
    array = jax.random.normal(rng, extent, jnp.float32) * scale
    return jnp.minimum(jnp.maximum(array, -limit), limit).astype(held_as)


def setup_inputs(seed: int = 0) -> dict:
    splits = jax.random.split(jax.random.key(seed), 6)
    object_slices = jnp.clip(jax.random.uniform(splits[0], (2, SLICES, NY, NX), jnp.float32, -1.0, 1.0) * block_scale(splits[0], (2, SLICES, NY, NX), ((2, 8), (3, 4)), -0.4, 0.0), -1.0, 1.0)
    positions = plant(jax.random.randint(splits[1], (N_ROW, N_COL, PROBES, 2), 0, CORE + 2 * HALO - W + 1), jax.random.fold_in(splits[1], 1), 0, CORE + 2 * HALO - W).astype(jnp.int32)
    intensities = jnp.clip(0.8 * jax.random.uniform(splits[2], (N_ROW, N_COL, PROBES, W, W), jnp.float32) ** block_scale(splits[2], (N_ROW, N_COL, PROBES, W, W), ((0, 8), (1, 4)), -0.2, 0.2), 0.0, 0.8)
    probe = bell_draw(splits[3], (2, W, W), 1.0, 6.0, jnp.float32)
    propagator = jnp.clip(jax.random.uniform(splits[4], (W, W), jnp.float32, -3.140625, 3.140625), -3.140625, 3.140625)
    return {"object_slices": object_slices, "positions": positions, "intensities": intensities, "probe": probe, "propagator": propagator}


descent_rate = 0.5

def tables(width):
    counter = jnp.arange(width, dtype=jnp.int32)
    product = counter[:, None] * counter[None, :] % width
    angles = product.astype(jnp.float32) * (2.0 * jnp.pi / width)
    norming = 1.0 / jnp.sqrt(jnp.float32(width))
    return (jnp.cos(angles) * norming, jnp.sin(angles) * norming)

def apply_left(matrix, field):
    return jnp.einsum('ab,kbc->kac', matrix, field, precision=lax.Precision.HIGHEST)

def apply_right(field, matrix):
    return jnp.einsum('kab,bc->kac', field, matrix, precision=lax.Precision.HIGHEST)

def fourier(real_part, imag_part, cosines, sines, direction):
    half_re = apply_left(cosines, real_part) - direction * apply_left(sines, imag_part)
    half_im = apply_left(cosines, imag_part) + direction * apply_left(sines, real_part)
    full_re = apply_right(half_re, cosines) - direction * apply_right(half_im, sines)
    full_im = apply_right(half_im, cosines) + direction * apply_right(half_re, sines)
    return (full_re, full_im)

def complex_product(left_re, left_im, right_re, right_im):
    return (left_re * right_re - left_im * right_im, left_re * right_im + left_im * right_re)

def probe_gradients(windows, probe, propagator, measured):
    width = probe.shape[-1]
    layers = windows.shape[2]
    count = windows.shape[0]
    cosines, sines = tables(width)
    phase_re = jnp.cos(propagator)
    phase_im = jnp.sin(propagator)
    wave_re = jnp.broadcast_to(probe[0], (count, width, width))
    wave_im = jnp.broadcast_to(probe[1], (count, width, width))
    stored = []
    for layer in range(layers):
        stored.append((wave_re, wave_im))
        exit_re, exit_im = complex_product(wave_re, wave_im, windows[:, 0, layer], windows[:, 1, layer])
        if layer < layers - 1:
            freq_re, freq_im = fourier(exit_re, exit_im, cosines, sines, -1.0)
            freq_re, freq_im = complex_product(freq_re, freq_im, phase_re, phase_im)
            wave_re, wave_im = fourier(freq_re, freq_im, cosines, sines, 1.0)
    far_re, far_im = fourier(exit_re, exit_im, cosines, sines, -1.0)
    misfit = far_re * far_re + far_im * far_im - measured
    back_re, back_im = fourier(misfit * far_re, misfit * far_im, cosines, sines, 1.0)
    real_terms = [None] * layers
    imag_terms = [None] * layers
    for layer in range(layers - 1, -1, -1):
        wave_re, wave_im = stored[layer]
        real_terms[layer] = wave_re * back_re + wave_im * back_im
        imag_terms[layer] = wave_re * back_im - wave_im * back_re
        if layer > 0:
            slab_re = windows[:, 0, layer]
            slab_im = windows[:, 1, layer]
            back_re, back_im = (slab_re * back_re + slab_im * back_im, slab_re * back_im - slab_im * back_re)
            freq_re, freq_im = fourier(back_re, back_im, cosines, sines, -1.0)
            freq_re, freq_im = complex_product(freq_re, freq_im, phase_re, -phase_im)
            back_re, back_im = fourier(freq_re, freq_im, cosines, sines, 1.0)
    real_stack = jnp.stack(real_terms, axis=1)
    imag_stack = jnp.stack(imag_terms, axis=1)
    return jnp.stack([real_stack, imag_stack], axis=1)

def reference(object_slices, positions, intensities, probe, propagator):
    total_rows = object_slices.shape[2]
    total_cols = object_slices.shape[3]
    width = probe.shape[-1]
    counter = jnp.arange(width, dtype=jnp.int32)

    def cut_window(row_index, col_index):
        return object_slices[:, :, row_index][:, :, :, col_index]

    def one_tile(gradient_sum, tile_index):
        tile_row = tile_index // N_COL
        tile_col = tile_index % N_COL
        offsets = positions[tile_row, tile_col]
        row_start = tile_row * CORE - HALO + offsets[:, 0]
        col_start = tile_col * CORE - HALO + offsets[:, 1]
        row_index = ((row_start[:, None] + counter[None, :]) % total_rows).astype(jnp.int32)
        col_index = ((col_start[:, None] + counter[None, :]) % total_cols).astype(jnp.int32)
        windows = jax.vmap(cut_window)(row_index, col_index)
        terms = probe_gradients(windows, probe, propagator, intensities[tile_row, tile_col])

        def add_one(index, running):
            return running.at[:, :, row_index[index][:, None], col_index[index][None, :]].add(terms[index])
        gradient_sum = lax.fori_loop(0, terms.shape[0], add_one, gradient_sum)
        return (gradient_sum, None)
    zeros = jnp.zeros_like(object_slices)
    gradient, _ = lax.scan(one_tile, zeros, jnp.arange(N_ROW * N_COL, dtype=jnp.int32))
    return (gradient, object_slices - descent_rate * gradient)
```

```python
import jax
import jax.numpy as jnp
import numpy as np
from jax import lax
from jax.experimental import pallas as pl
from jax.experimental.pallas import tpu as pltpu
from jax.sharding import PartitionSpec as P

HALO = 64


descent_rate = 0.5


def split(value):
    high = value.astype(jnp.bfloat16)
    low = (value - high.astype(jnp.float32)).astype(jnp.bfloat16)
    return high, low


def half_tables(width):
    half = width // 2
    place = np.arange(half)
    found = []
    for odd in (0, 1):
        angle = 2.0 * np.pi * (np.outer(2 * place + odd, place) % width) / width
        re = np.cos(angle) / np.sqrt(width)
        im = -np.sin(angle) / np.sqrt(width)
        found.append(np.block([[re, -im], [im, re]]).astype(np.float32))
    even, odd = found
    four = np.stack([even, odd, even.T, odd.T])
    high = four.astype(jnp.bfloat16)
    low = (four - high.astype(np.float32)).astype(jnp.bfloat16)
    lefts = np.concatenate([high, high, low], axis=2)
    rights = np.concatenate([np.swapaxes(high, 1, 2), np.swapaxes(high, 1, 2), np.swapaxes(low, 1, 2)], axis=1)
    return lefts, rights


def dot_left(matrix, value):
    high, low = split(value)
    return jnp.dot(matrix, jnp.concatenate([high, low, high], 0), preferred_element_type=jnp.float32)


def dot_right(value, matrix):
    high, low = split(value)
    return jnp.dot(jnp.concatenate([high, low, high], 1), matrix, preferred_element_type=jnp.float32)


def cut(value, dim):
    half = value.shape[dim] // 2
    return (lax.slice_in_dim(value, 0, half, axis=dim), lax.slice_in_dim(value, half, 2 * half, axis=dim))


def joined(first, second, dim):
    return jnp.concatenate([first, second], dim)


def forward_axis(re, im, dim, dot, even_matrix, odd_matrix):
    r0, r1 = cut(re, dim)
    i0, i1 = cut(im, dim)
    even_re, even_im = cut(dot(joined(r0 + r1, i0 + i1, dim), even_matrix), dim)
    odd_re, odd_im = cut(dot(joined(r0 - r1, i0 - i1, dim), odd_matrix), dim)
    return joined(even_re, odd_re, dim), joined(even_im, odd_im, dim)


def inverse_axis(re, im, dim, dot, even_matrix, odd_matrix):
    r0, r1 = cut(re, dim)
    i0, i1 = cut(im, dim)
    p_re, p_im = cut(dot(joined(r0, i0, dim), even_matrix), dim)
    q_re, q_im = cut(dot(joined(r1, i1, dim), odd_matrix), dim)
    return joined(p_re + q_re, p_re - q_re, dim), joined(p_im + q_im, p_im - q_im, dim)


def left_dot(value, matrix):
    return dot_left(matrix, value)


def forward(re, im, lefts, rights):
    re, im = forward_axis(re, im, 0, left_dot, lefts[0], lefts[1])
    return forward_axis(re, im, 1, dot_right, rights[0], rights[1])


def inverse(re, im, lefts, rights):
    re, im = inverse_axis(re, im, 1, dot_right, rights[2], rights[3])
    return inverse_axis(re, im, 0, left_dot, lefts[2], lefts[3])


def by_parity(array, dim):
    return jnp.concatenate(
        [
            lax.slice_in_dim(array, 0, array.shape[dim], stride=2, axis=dim),
            lax.slice_in_dim(array, 1, array.shape[dim], stride=2, axis=dim),
        ],
        axis=dim,
    )


def complex_product(left_re, left_im, right_re, right_im):
    return (left_re * right_re - left_im * right_im, left_re * right_im + left_im * right_re)


def slid(whole, shift, axis, span):
    turned = pltpu.roll(whole, lax.rem(span - shift, span), axis)
    kept = lax.broadcasted_iota(jnp.int32, whole[:-1].shape, axis) < span - shift
    return jnp.where(kept, turned[:-1], turned[1:])


def spread(whole, shift, axis, span):
    turned = pltpu.roll(whole, lax.rem(shift, span), axis)
    zero = jnp.zeros_like(turned[:1])
    first = jnp.concatenate([zero, turned], 0)
    other = jnp.concatenate([turned, zero], 0)
    moved = lax.broadcasted_iota(jnp.int32, first.shape, axis) < shift
    return jnp.where(moved, first, other)


def row_place(oy, rows, width):
    base = jnp.minimum(oy - lax.rem(oy, 8), rows - width - 8)
    return pl.ds(pl.multiple_of(base, 8), width + 8), oy - base


def lane_blocks(value):
    return jnp.stack([value[:, at : at + 128] for at in range(0, value.shape[1], 128)])


def lane_joined(blocks):
    return jnp.concatenate([blocks[i] for i in range(blocks.shape[0])], 1)


def take_window(whole, shift, ox):
    rows, lanes = whole.shape
    whole = slid(whole.reshape(rows // 8, 8, lanes), shift, 1, 8).reshape(rows - 8, lanes)
    return lane_joined(slid(lane_blocks(whole), ox, 2, 128))


def widened(term, shift, ox):
    term = lane_joined(spread(lane_blocks(term), ox, 2, 128))
    rows, lanes = term.shape
    return spread(term.reshape(rows // 8, 8, lanes), shift, 1, 8).reshape(rows + 8, lanes)


def step_kernel(offsets, ext, measured, probe, phase, lefts, rights, out, windows, waves):
    count = measured.shape[0]
    width = measured.shape[-1]
    layers = ext.shape[1]
    last = layers - 1
    out[...] = jnp.zeros_like(out)
    for k in range(count):
        waves[k, 0] = probe[...]

    def cut_layer(k, layer):
        rows, shift = row_place(offsets[k, 0], ext.shape[2], width)
        for c in range(2):
            windows[k, layer, c] = take_window(ext[c, layer, rows, :], shift, offsets[k, 1])

    def leave(k, layer):
        return complex_product(
            waves[k, layer, 0], waves[k, layer, 1], windows[k, layer, 0], windows[k, layer, 1]
        )

    def onward(layer, carry):
        for k in range(count):
            cut_layer(k, layer)
            re, im = forward(*leave(k, layer), lefts, rights)
            re, im = complex_product(re, im, phase[0], phase[1])
            re, im = inverse(re, im, lefts, rights)
            waves[k, layer + 1, 0] = re
            waves[k, layer + 1, 1] = im
        return carry

    lax.fori_loop(0, last, onward, 0)

    def record(k, layer, back_re, back_im):
        wave_re, wave_im = waves[k, layer, 0], waves[k, layer, 1]
        rows, shift = row_place(offsets[k, 0], ext.shape[2], width)
        re_term = wave_re * back_re + wave_im * back_im
        im_term = wave_re * back_im - wave_im * back_re
        out[0, layer, rows, :] += widened(re_term, shift, offsets[k, 1])
        out[1, layer, rows, :] += widened(im_term, shift, offsets[k, 1])

    for k in range(count):
        cut_layer(k, last)
        far_re, far_im = forward(*leave(k, last), lefts, rights)
        misfit = far_re * far_re + far_im * far_im - measured[k]
        back_re, back_im = inverse(misfit * far_re, misfit * far_im, lefts, rights)
        record(k, last, back_re, back_im)
        waves[k, last, 0] = back_re
        waves[k, last, 1] = back_im

    def backward(step, carry):
        layer = last - step
        for k in range(count):
            back_re, back_im = waves[k, layer, 0], waves[k, layer, 1]
            slab_re, slab_im = windows[k, layer, 0], windows[k, layer, 1]
            re, im = complex_product(back_re, back_im, slab_re, -slab_im)
            re, im = forward(re, im, lefts, rights)
            re, im = complex_product(re, im, phase[0], -phase[1])
            re, im = inverse(re, im, lefts, rights)
            record(k, layer - 1, re, im)
            waves[k, layer - 1, 0] = re
            waves[k, layer - 1, 1] = im
        return carry

    lax.fori_loop(0, last, backward, 0)


def window_sums(extended, offsets, measured, probe, propagator):
    count = measured.shape[0]
    width = measured.shape[-1]
    layers = extended.shape[1]
    lefts, rights = half_tables(width)
    ordered = by_parity(by_parity(propagator, 0), 1)
    phase = jnp.stack([jnp.cos(ordered), jnp.sin(ordered)])
    measured = by_parity(by_parity(measured, 1), 2)
    vmem = pl.BlockSpec(memory_space=pltpu.VMEM)
    return pl.pallas_call(
        step_kernel,
        out_shape=jax.ShapeDtypeStruct(extended.shape, jnp.float32),
        in_specs=[pl.BlockSpec(memory_space=pltpu.SMEM)] + [vmem] * 6,
        out_specs=vmem,
        scratch_shapes=[
            pltpu.VMEM((count, layers, 2, width, width), jnp.float32),
            pltpu.VMEM((count, layers, 2, width, width), jnp.float32),
        ],
        compiler_params=pltpu.CompilerParams(vmem_limit_bytes=50 * 2**20),
    )(offsets, extended, measured, probe, phase, jnp.asarray(lefts), jnp.asarray(rights))


def passed_along(block, axis, distance):
    devices = range(lax.axis_size(axis))
    route = [((i - distance) % len(devices), i) for i in devices]
    return lax.ppermute(block, axis, route)


def with_halo(cells, sides, width):
    for axis, dim in sides:
        count = lax.axis_size(axis)
        head = lax.slice_in_dim(cells, 0, width, axis=dim)
        tail = lax.slice_in_dim(cells, cells.shape[dim] - width, cells.shape[dim], axis=dim)
        cells = jnp.concatenate(
            [
                lax.ppermute(tail, axis, [(i, (i + 1) % count) for i in range(count)]),
                cells,
                lax.ppermute(head, axis, [((i + 1) % count, i) for i in range(count)]),
            ],
            axis=dim,
        )
    return cells


def fold_rows(summed):
    extent = summed.shape[2]
    inner = extent - 2 * HALO
    from_below = passed_along(summed[:, :, :HALO], "row", -1)
    from_above = passed_along(summed[:, :, extent - HALO :], "row", 1)
    middle = summed[:, :, HALO : extent - HALO]
    middle = middle.at[:, :, inner - HALO :].add(from_below)
    return middle.at[:, :, :HALO].add(from_above)


def fold_cols(summed):
    extent = summed.shape[3]
    inner = extent - 2 * HALO
    from_right = passed_along(summed[:, :, :, :HALO], "col", -1)
    from_left = passed_along(summed[:, :, :, extent - HALO :], "col", 1)
    middle = summed[:, :, :, HALO : extent - HALO]
    middle = middle.at[:, :, :, inner - HALO :].add(from_right)
    return middle.at[:, :, :, :HALO].add(from_left)


def on_device(object_slices, positions, intensities, probe, propagator):
    extended = with_halo(object_slices, (("row", 2), ("col", 3)), HALO)
    summed = window_sums(extended, positions[0, 0], intensities[0, 0], probe, propagator)
    gradient = fold_cols(fold_rows(summed))
    return (gradient, object_slices - descent_rate * gradient)


def solution(mesh):
    return jax.shard_map(
        on_device,
        mesh=mesh,
        in_specs=(
            P(None, None, "row", "col"),
            P("row", "col", None, None),
            P("row", "col", None, None, None),
            P(),
            P(),
        ),
        out_specs=(P(None, None, "row", "col"), P(None, None, "row", "col")),
        check_vma=False,
    )
```

```python
import jax
import jax.numpy as jnp
import numpy as np
from jax import lax
from jax.experimental import pallas as pl
from jax.experimental.pallas import tpu as pltpu
from jax.sharding import PartitionSpec as P

HALO = 64


descent_rate = 0.5


def passed_along(block, axis, distance):
    devices = range(lax.axis_size(axis))
    route = [((i - distance) % len(devices), i) for i in devices]
    return lax.ppermute(block, axis, route)


def split(value):
    high = value.astype(jnp.bfloat16)
    low = (value - high.astype(jnp.float32)).astype(jnp.bfloat16)
    return high, low


def half_tables(width):
    half = width // 2
    place = np.arange(half)
    found = []
    for odd in (0, 1):
        angle = 2.0 * np.pi * (np.outer(2 * place + odd, place) % width) / width
        re = np.cos(angle) / np.sqrt(width)
        im = -np.sin(angle) / np.sqrt(width)
        found.append(np.block([[re, -im], [im, re]]).astype(np.float32))
    even, odd = found
    order = np.eye(width, dtype=np.float32)[np.concatenate([2 * place, 2 * place + 1])]
    six = np.stack([even, odd, even.T, odd.T, order, order.T])
    high = six.astype(jnp.bfloat16)
    low = (six - high.astype(np.float32)).astype(jnp.bfloat16)
    return np.stack([high, low])


def dot_left(pair, value):
    high, low = split(value)
    matrix = jnp.concatenate([pair[0], pair[0], pair[1]], 1)
    return jnp.dot(matrix, jnp.concatenate([high, low, high], 0), preferred_element_type=jnp.float32)


def dot_right(value, pair):
    high, low = split(value)
    matrix = jnp.concatenate([pair[0], pair[0], pair[1]], 0)
    return jnp.dot(jnp.concatenate([high, low, high], 1), matrix, preferred_element_type=jnp.float32)


def cut(value, dim):
    half = value.shape[dim] // 2
    return (lax.slice_in_dim(value, 0, half, axis=dim), lax.slice_in_dim(value, half, 2 * half, axis=dim))


def joined(first, second, dim):
    return jnp.concatenate([first, second], dim)


def forward_axis(re, im, dim, dot, even_matrix, odd_matrix):
    r0, r1 = cut(re, dim)
    i0, i1 = cut(im, dim)
    even_re, even_im = cut(dot(joined(r0 + r1, i0 + i1, dim), even_matrix), dim)
    odd_re, odd_im = cut(dot(joined(r0 - r1, i0 - i1, dim), odd_matrix), dim)
    return joined(even_re, odd_re, dim), joined(even_im, odd_im, dim)


def inverse_axis(re, im, dim, dot, even_matrix, odd_matrix):
    r0, r1 = cut(re, dim)
    i0, i1 = cut(im, dim)
    p_re, p_im = cut(dot(joined(r0, i0, dim), even_matrix), dim)
    q_re, q_im = cut(dot(joined(r1, i1, dim), odd_matrix), dim)
    return joined(p_re + q_re, p_re - q_re, dim), joined(p_im + q_im, p_im - q_im, dim)


def left_dot(value, pair):
    return dot_left(pair, value)


def forward(re, im, pairs):
    re, im = forward_axis(re, im, 0, left_dot, pairs(0), pairs(1))
    return forward_axis(re, im, 1, dot_right, pairs(2), pairs(3))


def inverse(re, im, pairs):
    re, im = inverse_axis(re, im, 1, dot_right, pairs(0), pairs(1))
    return inverse_axis(re, im, 0, left_dot, pairs(2), pairs(3))


def by_parity(value, pairs):
    return dot_right(dot_left(pairs(4), value), pairs(5))


def complex_product(left_re, left_im, right_re, right_im):
    return (left_re * right_re - left_im * right_im, left_re * right_im + left_im * right_re)


def slid(whole, shift, axis, span):
    turned = pltpu.roll(whole, lax.rem(span - shift, span), axis)
    kept = lax.broadcasted_iota(jnp.int32, whole[:-1].shape, axis) < span - shift
    return jnp.where(kept, turned[:-1], turned[1:])


def spread(whole, shift, axis, span):
    turned = pltpu.roll(whole, lax.rem(shift, span), axis)
    zero = jnp.zeros_like(turned[:1])
    first = jnp.concatenate([zero, turned], 0)
    other = jnp.concatenate([turned, zero], 0)
    moved = lax.broadcasted_iota(jnp.int32, first.shape, axis) < shift
    return jnp.where(moved, first, other)


def row_place(oy, rows, width):
    base = jnp.minimum(oy - lax.rem(oy, 8), rows - width - 8)
    return pl.ds(pl.multiple_of(base, 8), width + 8), oy - base


def lane_place(ox, lanes=128):
    early = ox < HALO
    return jnp.where(early, 2, 0), jnp.where(early, ox + lanes - HALO, ox - HALO)


def swapped(value):
    return pltpu.roll(value, HALO, value.ndim - 1)


def lower_lanes(value):
    return lax.broadcasted_iota(jnp.int32, value.shape, value.ndim - 1) < HALO


def step_kernel(
    offsets, core, edges, right, left, right_ends, left_ends, measured, probe, phase, tables,
    out, out_edges, to_right, to_left, to_right_ends, to_left_ends,
    ext, total, windows, waves, ordered, phases,
):
    count = measured.shape[0]
    width = measured.shape[-1]
    layers = core.shape[1]
    last = layers - 1
    tall = core.shape[2]
    wide = core.shape[3] // 128
    rounds = wide + 1
    whole = tall + 2 * HALO
    pieces = ((0, HALO, True, 0), (HALO, tall, False, 0), (HALO + tall, HALO, True, HALO))

    def pairs(index):
        return tables[0, index], tables[1, index]

    def gather(layer, carry):
        for start, size, is_edge, at in pieces:
            rows, own = pl.ds(start, size), pl.ds(at, size)
            for c in range(2):
                source = edges if is_edge else core
                for j in range(wide):
                    ext[c, layer, j, rows, :] = source[c, layer, own, pl.ds(j * 128, 128)]
            r = (right_ends if is_edge else right)[layer, own, :]
            l = (left_ends if is_edge else left)[layer, own, :]
            low = lower_lanes(r)
            ext[0, layer, wide, rows, :] = jnp.where(low, r, swapped(l))
            ext[1, layer, wide, rows, :] = jnp.where(low, swapped(r), l)
        return carry

    lax.fori_loop(0, layers, gather, 0)
    total[...] = jnp.zeros_like(total)
    for c in range(2):
        phases[c] = by_parity(phase[c], pairs)
    for k in range(count):
        waves[k, 0] = probe[...]
        ordered[k] = by_parity(measured[k], pairs)

    def cut_layer(k, layer):
        rows, shift = row_place(offsets[k, 0], whole, width)
        first, turn = lane_place(offsets[k, 1])
        for c in range(2):
            blocks = jnp.stack(
                [ext[c, layer, lax.rem(first + j, rounds), rows, :] for j in range(rounds)]
            )
            blocks = slid(blocks, turn, 2, 128)
            for j in range(wide):
                part = blocks[j].reshape((width + 8) // 8, 8, 128)
                windows[k, layer, c, :, j * 128 : j * 128 + 128] = slid(part, shift, 1, 8).reshape(width, 128)

    def leave(k, layer):
        return complex_product(
            waves[k, layer, 0], waves[k, layer, 1], windows[k, layer, 0], windows[k, layer, 1]
        )

    def onward(layer, carry):
        for k in range(count):
            cut_layer(k, layer)
            re, im = forward(*leave(k, layer), pairs)
            re, im = complex_product(re, im, phases[0], phases[1])
            re, im = inverse(re, im, pairs)
            waves[k, layer + 1, 0] = re
            waves[k, layer + 1, 1] = im
        return carry

    lax.fori_loop(0, last, onward, 0)

    def record(k, layer, back_re, back_im):
        wave_re, wave_im = waves[k, layer, 0], waves[k, layer, 1]
        rows, shift = row_place(offsets[k, 0], whole, width)
        first, turn = lane_place(offsets[k, 1])
        terms = (wave_re * back_re + wave_im * back_im, wave_re * back_im - wave_im * back_re)
        for c in range(2):
            blocks = jnp.stack([terms[c][:, j * 128 : j * 128 + 128] for j in range(wide)])
            blocks = spread(blocks, turn, 2, 128)
            for j in range(rounds):
                part = spread(blocks[j].reshape(width // 8, 8, 128), shift, 1, 8)
                total[c, layer, lax.rem(first + j, rounds), rows, :] += part.reshape(width + 8, 128)

    for k in range(count):
        cut_layer(k, last)
        far_re, far_im = forward(*leave(k, last), pairs)
        misfit = far_re * far_re + far_im * far_im - ordered[k]
        back_re, back_im = inverse(misfit * far_re, misfit * far_im, pairs)
        record(k, last, back_re, back_im)
        waves[k, last, 0] = back_re
        waves[k, last, 1] = back_im

    def backward(step, carry):
        layer = last - step
        for k in range(count):
            back_re, back_im = waves[k, layer, 0], waves[k, layer, 1]
            slab_re, slab_im = windows[k, layer, 0], windows[k, layer, 1]
            re, im = complex_product(back_re, back_im, slab_re, -slab_im)
            re, im = forward(re, im, pairs)
            re, im = complex_product(re, im, phases[0], -phases[1])
            re, im = inverse(re, im, pairs)
            record(k, layer - 1, re, im)
            waves[k, layer - 1, 0] = re
            waves[k, layer - 1, 1] = im
        return carry

    lax.fori_loop(0, last, backward, 0)

    def hand_out(layer, carry):
        for start, size, is_edge, at in pieces:
            rows, own = pl.ds(start, size), pl.ds(at, size)
            for c in range(2):
                target = out_edges if is_edge else out
                for j in range(wide):
                    target[c, layer, own, pl.ds(j * 128, 128)] = total[c, layer, j, rows, :]
            re, im = total[0, layer, wide, rows, :], total[1, layer, wide, rows, :]
            low = lower_lanes(re)
            (to_right_ends if is_edge else to_right)[layer, own, :] = jnp.where(low, re, swapped(im))
            (to_left_ends if is_edge else to_left)[layer, own, :] = jnp.where(low, swapped(re), im)
        return carry

    lax.fori_loop(0, layers, hand_out, 0)


def packed(cells):
    wide = cells.shape[-1]
    head = jnp.concatenate([cells[0, ..., :HALO], cells[1, ..., :HALO]], -1)
    tail = jnp.concatenate([cells[0, ..., wide - HALO :], cells[1, ..., wide - HALO :]], -1)
    return head, tail


def like(array):
    return jax.ShapeDtypeStruct(array.shape, array.dtype)


def absorb(parts, cells, from_left, from_right):
    wide = cells.shape[-1]
    l, r = from_left[...], from_right[...]
    low = lower_lanes(l)
    zero = jnp.zeros_like(l)
    added = (
        (jnp.where(low, l, zero), jnp.where(low, zero, swapped(r))),
        (jnp.where(low, swapped(l), zero), jnp.where(low, zero, r)),
    )
    for c in range(2):
        parts[c, :, :, 0:128] = cells[c, :, :, 0:128] + added[c][0]
        for at in range(128, wide - 128, 128):
            parts[c, :, :, at : at + 128] = cells[c, :, :, at : at + 128]
        parts[c, :, :, wide - 128 : wide] = cells[c, :, :, wide - 128 : wide] + added[c][1]


def edges_kernel(edges, from_left, from_right, up, down):
    size = edges.shape[2] // 2
    top, bottom = pl.ds(0, size), pl.ds(size, size)
    absorb(up, edges.at[:, :, top, :], from_left.at[:, top, :], from_right.at[:, top, :])
    absorb(down, edges.at[:, :, bottom, :], from_left.at[:, bottom, :], from_right.at[:, bottom, :])


def final_kernel(cells, from_left, from_right, from_above, from_below, objects, gradient, updated):
    tall = cells.shape[2]
    absorb(gradient, cells, from_left, from_right)
    gradient[:, :, 0:HALO, :] += from_above[...]
    gradient[:, :, tall - HALO : tall, :] += from_below[...]
    updated[...] = objects[...] - descent_rate * gradient[...]


def on_device(object_slices, positions, intensities, probe, propagator):
    measured = intensities[0, 0]
    count, width = measured.shape[0], measured.shape[-1]
    layers, tall, broad = object_slices.shape[1:]
    wide = broad // 128
    tables = jnp.asarray(half_tables(width))
    phase = jnp.stack([jnp.cos(propagator), jnp.sin(propagator)])
    above = passed_along(object_slices[:, :, tall - HALO :], "row", 1)
    below = passed_along(object_slices[:, :, :HALO], "row", -1)
    head, tail = packed(object_slices)
    right = passed_along(head, "col", -1)
    left = passed_along(tail, "col", 1)
    edges = jnp.concatenate([above, below], 2)
    head, tail = packed(edges)
    right_ends = passed_along(head, "col", -1)
    left_ends = passed_along(tail, "col", 1)
    vmem = pl.BlockSpec(memory_space=pltpu.VMEM)
    limit = pltpu.CompilerParams(vmem_limit_bytes=58 * 2**20)
    cells, edges, to_right, to_left, to_right_ends, to_left_ends = pl.pallas_call(
        step_kernel,
        out_shape=[like(v) for v in (object_slices, edges, right, left, right_ends, left_ends)],
        in_specs=[pl.BlockSpec(memory_space=pltpu.SMEM)] + [vmem] * 10,
        out_specs=[vmem] * 6,
        scratch_shapes=[
            pltpu.VMEM((2, layers, wide + 1, tall + 2 * HALO, 128), jnp.float32),
            pltpu.VMEM((2, layers, wide + 1, tall + 2 * HALO, 128), jnp.float32),
            pltpu.VMEM((count, layers, 2, width, width), jnp.float32),
            pltpu.VMEM((count, layers, 2, width, width), jnp.float32),
            pltpu.VMEM((count, width, width), jnp.float32),
            pltpu.VMEM((2, width, width), jnp.float32),
        ],
        compiler_params=limit,
    )(
        positions[0, 0], object_slices, edges, right, left, right_ends, left_ends,
        measured, probe, phase, tables,
    )
    left_ends = passed_along(to_right_ends, "col", 1)
    right_ends = passed_along(to_left_ends, "col", -1)
    left = passed_along(to_right, "col", 1)
    right = passed_along(to_left, "col", -1)
    up, down = pl.pallas_call(
        edges_kernel,
        out_shape=[like(above), like(below)],
        in_specs=[vmem] * 3,
        out_specs=[vmem] * 2,
        compiler_params=limit,
    )(edges, left_ends, right_ends)
    from_above = passed_along(down, "row", 1)
    from_below = passed_along(up, "row", -1)
    return tuple(
        pl.pallas_call(
            final_kernel,
            out_shape=[like(cells), like(cells)],
            in_specs=[vmem] * 6,
            out_specs=[vmem] * 2,
            compiler_params=limit,
        )(cells, left, right, from_above, from_below, object_slices)
    )


def solution(mesh):
    return jax.shard_map(
        on_device,
        mesh=mesh,
        in_specs=(
            P(None, None, "row", "col"),
            P("row", "col", None, None),
            P("row", "col", None, None, None),
            P(),
            P(),
        ),
        out_specs=(P(None, None, "row", "col"), P(None, None, "row", "col")),
        check_vma=False,
    )
```

```python
import jax
import jax.numpy as jnp
import numpy as np
from jax import lax
from jax.experimental import pallas as pl
from jax.experimental.pallas import tpu as pltpu
from jax.sharding import PartitionSpec as P

HALO = 64


descent_rate = 0.5


def passed_along(block, axis, distance):
    devices = range(lax.axis_size(axis))
    route = [((i - distance) % len(devices), i) for i in devices]
    return lax.ppermute(block, axis, route)


def split(value):
    high = value.astype(jnp.bfloat16)
    low = (value - high.astype(jnp.float32)).astype(jnp.bfloat16)
    return high, low


def half_tables(width):
    half = width // 2
    place = np.arange(half)
    found = []
    for odd in (0, 1):
        angle = 2.0 * np.pi * (np.outer(2 * place + odd, place) % width) / width
        re = np.cos(angle) / np.sqrt(width)
        im = -np.sin(angle) / np.sqrt(width)
        found.append(np.block([[re, -im], [im, re]]).astype(np.float32))
    even, odd = found
    order = np.eye(width, dtype=np.float32)[np.concatenate([2 * place, 2 * place + 1])]
    six = np.stack([even, odd, even.T, odd.T, order, order.T])
    high = six.astype(jnp.bfloat16)
    low = (six - high.astype(np.float32)).astype(jnp.bfloat16)
    return np.stack([high, low])


def dot_left(pair, value):
    high, low = split(value)
    matrix = jnp.concatenate([pair[0], pair[0], pair[1]], 1)
    return jnp.dot(matrix, jnp.concatenate([high, low, high], 0), preferred_element_type=jnp.float32)


def dot_right(value, pair):
    high, low = split(value)
    matrix = jnp.concatenate([pair[0], pair[0], pair[1]], 0)
    return jnp.dot(jnp.concatenate([high, low, high], 1), matrix, preferred_element_type=jnp.float32)


def cut(value, dim):
    half = value.shape[dim] // 2
    return (lax.slice_in_dim(value, 0, half, axis=dim), lax.slice_in_dim(value, half, 2 * half, axis=dim))


def joined(first, second, dim):
    return jnp.concatenate([first, second], dim)


def forward_axis(re, im, dim, dot, even_matrix, odd_matrix):
    r0, r1 = cut(re, dim)
    i0, i1 = cut(im, dim)
    even_re, even_im = cut(dot(joined(r0 + r1, i0 + i1, dim), even_matrix), dim)
    odd_re, odd_im = cut(dot(joined(r0 - r1, i0 - i1, dim), odd_matrix), dim)
    return joined(even_re, odd_re, dim), joined(even_im, odd_im, dim)


def inverse_axis(re, im, dim, dot, even_matrix, odd_matrix):
    r0, r1 = cut(re, dim)
    i0, i1 = cut(im, dim)
    p_re, p_im = cut(dot(joined(r0, i0, dim), even_matrix), dim)
    q_re, q_im = cut(dot(joined(r1, i1, dim), odd_matrix), dim)
    return joined(p_re + q_re, p_re - q_re, dim), joined(p_im + q_im, p_im - q_im, dim)


def left_dot(value, pair):
    return dot_left(pair, value)


def forward(re, im, pairs):
    re, im = forward_axis(re, im, 0, left_dot, pairs(0), pairs(1))
    return forward_axis(re, im, 1, dot_right, pairs(2), pairs(3))


def inverse(re, im, pairs):
    re, im = inverse_axis(re, im, 1, dot_right, pairs(0), pairs(1))
    return inverse_axis(re, im, 0, left_dot, pairs(2), pairs(3))


def by_parity(value, pairs):
    return dot_right(dot_left(pairs(4), value), pairs(5))


def complex_product(left_re, left_im, right_re, right_im):
    return (left_re * right_re - left_im * right_im, left_re * right_im + left_im * right_re)


def slid(whole, shift, axis, span):
    turned = pltpu.roll(whole, lax.rem(span - shift, span), axis)
    kept = lax.broadcasted_iota(jnp.int32, whole[:-1].shape, axis) < span - shift
    return jnp.where(kept, turned[:-1], turned[1:])


def spread(whole, shift, axis, span):
    turned = pltpu.roll(whole, lax.rem(shift, span), axis)
    zero = jnp.zeros_like(turned[:1])
    first = jnp.concatenate([zero, turned], 0)
    other = jnp.concatenate([turned, zero], 0)
    moved = lax.broadcasted_iota(jnp.int32, first.shape, axis) < shift
    return jnp.where(moved, first, other)


def row_place(oy, rows, width):
    base = jnp.minimum(oy - lax.rem(oy, 8), rows - width - 8)
    return pl.ds(pl.multiple_of(base, 8), width + 8), oy - base


def lane_place(ox, lanes=128):
    early = ox < HALO
    return jnp.where(early, 2, 0), jnp.where(early, ox + lanes - HALO, ox - HALO)


def swapped(value):
    return pltpu.roll(value, HALO, value.ndim - 1)


def lower_lanes(value):
    return lax.broadcasted_iota(jnp.int32, value.shape, value.ndim - 1) < HALO


def row_pieces(tall):
    return ((0, HALO, True, 0), (HALO, tall, False, 0), (HALO + tall, HALO, True, HALO))


def fill_ext(ext, core, edges, right, left, right_ends, left_ends):
    wide = core.shape[3] // 128

    def gather(layer, carry):
        for start, size, is_edge, at in row_pieces(core.shape[2]):
            rows, own = pl.ds(start, size), pl.ds(at, size)
            for c in range(2):
                source = edges if is_edge else core
                for j in range(wide):
                    ext[c, layer, j, rows, :] = source[c, layer, own, pl.ds(j * 128, 128)]
            r = (right_ends if is_edge else right)[layer, own, :]
            l = (left_ends if is_edge else left)[layer, own, :]
            low = lower_lanes(r)
            ext[0, layer, wide, rows, :] = jnp.where(low, r, swapped(l))
            ext[1, layer, wide, rows, :] = jnp.where(low, swapped(r), l)
        return carry

    lax.fori_loop(0, core.shape[1], gather, 0)


def cut_layer(ext, windows, offsets, k, layer):
    rounds, whole = ext.shape[2], ext.shape[3]
    width = windows.shape[-1]
    rows, shift = row_place(offsets[k, 0], whole, width)
    first, turn = lane_place(offsets[k, 1])
    for c in range(2):
        blocks = jnp.stack([ext[c, layer, lax.rem(first + j, rounds), rows, :] for j in range(rounds)])
        blocks = slid(blocks, turn, 2, 128)
        for j in range(rounds - 1):
            part = blocks[j].reshape((width + 8) // 8, 8, 128)
            windows[k, layer, c, :, j * 128 : j * 128 + 128] = slid(part, shift, 1, 8).reshape(width, 128)


def leave(waves, windows, k, layer):
    return complex_product(
        waves[k, layer, 0], waves[k, layer, 1], windows[k, layer, 0], windows[k, layer, 1]
    )


def hop(re, im, phases, sign, pairs):
    re, im = forward(re, im, pairs)
    re, im = complex_product(re, im, phases[0], sign * phases[1])
    return inverse(re, im, pairs)


def onward(ext, windows, waves, offsets, phases, pairs, steps):
    def one(layer, carry):
        for k in range(waves.shape[0]):
            cut_layer(ext, windows, offsets, k, layer)
            re, im = hop(*leave(waves, windows, k, layer), phases, 1.0, pairs)
            waves[k, layer + 1, 0] = re
            waves[k, layer + 1, 1] = im
        return carry

    lax.fori_loop(0, steps, one, 0)


def record(total, waves, offsets, k, layer, back_re, back_im):
    rounds, whole = total.shape[2], total.shape[3]
    width = waves.shape[-1]
    wave_re, wave_im = waves[k, layer, 0], waves[k, layer, 1]
    rows, shift = row_place(offsets[k, 0], whole, width)
    first, turn = lane_place(offsets[k, 1])
    terms = (wave_re * back_re + wave_im * back_im, wave_re * back_im - wave_im * back_re)
    for c in range(2):
        blocks = jnp.stack([terms[c][:, j * 128 : j * 128 + 128] for j in range(rounds - 1)])
        blocks = spread(blocks, turn, 2, 128)
        for j in range(rounds):
            part = spread(blocks[j].reshape(width // 8, 8, 128), shift, 1, 8)
            total[c, layer, lax.rem(first + j, rounds), rows, :] += part.reshape(width + 8, 128)


def returned(back, windows, k, layer):
    return complex_product(back[k, 0], back[k, 1], windows[k, layer, 0], -windows[k, layer, 1])


def backward(total, windows, waves, back, offsets, phases, pairs, start):
    def one(step, carry):
        layer = start - step
        for k in range(waves.shape[0]):
            re, im = hop(*returned(back, windows, k, layer), phases, -1.0, pairs)
            record(total, waves, offsets, k, layer - 1, re, im)
            back[k, 0] = re
            back[k, 1] = im
        return carry

    lax.fori_loop(0, start, one, 0)


def hand_out(total, out, out_edges, to_right, to_left, to_right_ends, to_left_ends):
    wide = out.shape[3] // 128

    def one(layer, carry):
        for start, size, is_edge, at in row_pieces(out.shape[2]):
            rows, own = pl.ds(start, size), pl.ds(at, size)
            for c in range(2):
                target = out_edges if is_edge else out
                for j in range(wide):
                    target[c, layer, own, pl.ds(j * 128, 128)] = total[c, layer, j, rows, :]
            re, im = total[0, layer, wide, rows, :], total[1, layer, wide, rows, :]
            low = lower_lanes(re)
            (to_right_ends if is_edge else to_right)[layer, own, :] = jnp.where(low, re, swapped(im))
            (to_left_ends if is_edge else to_left)[layer, own, :] = jnp.where(low, swapped(re), im)
        return carry

    lax.fori_loop(0, out.shape[1], one, 0)


def table_pairs(tables):
    return lambda index: (tables[0, index], tables[1, index])


def entry_kernel(measured, phase, tables, ordered, phases):
    pairs = table_pairs(tables)
    for c in range(2):
        phases[c] = by_parity(phase[c], pairs)
    for k in range(measured.shape[0]):
        ordered[k] = by_parity(measured[k], pairs)


def first_kernel(offsets, *refs):
    pieces, (probe, phases, tables, waves, windows, ext) = refs[:6], refs[6:]
    fill_ext(ext, *pieces)
    for k in range(waves.shape[0]):
        waves[k, 0] = probe[...]
    onward(ext, windows, waves, offsets, phases, table_pairs(tables), windows.shape[1])


def turn_kernel(offsets, *refs):
    pieces, (entering, ordered, phases, tables) = refs[:6], refs[6:10]
    outs, slab_back, (ext, total, waves, windows, back) = refs[10:16], refs[16], refs[17:]
    pairs = table_pairs(tables)
    last = windows.shape[1] - 1
    fill_ext(ext, *pieces)
    total[...] = jnp.zeros_like(total)
    for k in range(waves.shape[0]):
        waves[k, 0] = entering[k, entering.shape[1] - 1]
    onward(ext, windows, waves, offsets, phases, pairs, last)
    for k in range(waves.shape[0]):
        cut_layer(ext, windows, offsets, k, last)
        far_re, far_im = forward(*leave(waves, windows, k, last), pairs)
        misfit = far_re * far_re + far_im * far_im - ordered[k]
        re, im = inverse(misfit * far_re, misfit * far_im, pairs)
        record(total, waves, offsets, k, last, re, im)
        back[k, 0] = re
        back[k, 1] = im
    backward(total, windows, waves, back, offsets, phases, pairs, last)
    for k in range(waves.shape[0]):
        re, im = returned(back, windows, k, 0)
        slab_back[k, 0] = re
        slab_back[k, 1] = im
    hand_out(total, *outs)


def last_kernel(offsets, waves, windows, slab_back, phases, tables, *refs):
    outs, (total, back) = refs[:6], refs[6:]
    pairs = table_pairs(tables)
    start = windows.shape[1] - 1
    total[...] = jnp.zeros_like(total)
    for k in range(waves.shape[0]):
        re, im = hop(slab_back[k, 0], slab_back[k, 1], phases, -1.0, pairs)
        record(total, waves, offsets, k, start, re, im)
        back[k, 0] = re
        back[k, 1] = im
    backward(total, windows, waves, back, offsets, phases, pairs, start)
    hand_out(total, *outs)


def packed(cells):
    wide = cells.shape[-1]
    head = jnp.concatenate([cells[0, ..., :HALO], cells[1, ..., :HALO]], -1)
    tail = jnp.concatenate([cells[0, ..., wide - HALO :], cells[1, ..., wide - HALO :]], -1)
    return head, tail


def like(array):
    return jax.ShapeDtypeStruct(array.shape, array.dtype)


def absorb(parts, cells, from_left, from_right):
    wide = cells.shape[-1]
    l, r = from_left[...], from_right[...]
    low = lower_lanes(l)
    zero = jnp.zeros_like(l)
    added = (
        (jnp.where(low, l, zero), jnp.where(low, zero, swapped(r))),
        (jnp.where(low, swapped(l), zero), jnp.where(low, zero, r)),
    )
    for c in range(2):
        parts[c, :, :, 0:128] = cells[c, :, :, 0:128] + added[c][0]
        for at in range(128, wide - 128, 128):
            parts[c, :, :, at : at + 128] = cells[c, :, :, at : at + 128]
        parts[c, :, :, wide - 128 : wide] = cells[c, :, :, wide - 128 : wide] + added[c][1]


def edges_kernel(edges, from_left, from_right, up, down):
    size = edges.shape[2] // 2
    top, bottom = pl.ds(0, size), pl.ds(size, size)
    absorb(up, edges.at[:, :, top, :], from_left.at[:, top, :], from_right.at[:, top, :])
    absorb(down, edges.at[:, :, bottom, :], from_left.at[:, bottom, :], from_right.at[:, bottom, :])


def final_kernel(*refs):
    groups, objects, gradient, updated = refs[:-3], refs[-3], refs[-2], refs[-1]
    at = 0
    for g in range(0, len(groups), 5):
        cells, from_left, from_right, from_above, from_below = groups[g : g + 5]
        tall = cells.shape[2]
        own = gradient.at[:, at : at + cells.shape[1]]
        absorb(own, cells, from_left, from_right)
        own[:, :, 0:HALO, :] += from_above[...]
        own[:, :, tall - HALO : tall, :] += from_below[...]
        at += cells.shape[1]
    updated[...] = objects[...] - descent_rate * gradient[...]


def gathered(cells):
    tall = cells.shape[2]
    above = passed_along(cells[:, :, tall - HALO :], "row", 1)
    below = passed_along(cells[:, :, :HALO], "row", -1)
    head, tail = packed(cells)
    right = passed_along(head, "col", -1)
    left = passed_along(tail, "col", 1)
    edges = jnp.concatenate([above, below], 2)
    head, tail = packed(edges)
    return (cells, edges, right, left, passed_along(head, "col", -1), passed_along(tail, "col", 1))


def folded(cells, edges, to_right, to_left, to_right_ends, to_left_ends):
    left_ends = passed_along(to_right_ends, "col", 1)
    right_ends = passed_along(to_left_ends, "col", -1)
    left = passed_along(to_right, "col", 1)
    right = passed_along(to_left, "col", -1)
    shape = list(edges.shape)
    shape[2] //= 2
    part = jax.ShapeDtypeStruct(tuple(shape), edges.dtype)
    up, down = called(edges_kernel, [part, part], [], 0)(edges, left_ends, right_ends)
    return (cells, left, right, passed_along(down, "row", 1), passed_along(up, "row", -1))


def called(kernel, outs, scratch, hops, scalars=0):
    vmem = pl.BlockSpec(memory_space=pltpu.VMEM)
    smem = pl.BlockSpec(memory_space=pltpu.SMEM)

    def call(*operands):
        moved = sum(4 * v.size for v in outs) + sum(4 * v.size for v in operands)
        return pl.pallas_call(
            kernel,
            out_shape=outs,
            in_specs=[smem] * scalars + [vmem] * (len(operands) - scalars),
            out_specs=[vmem] * len(outs),
            scratch_shapes=[pltpu.VMEM(shape, jnp.float32) for shape in scratch],
            compiler_params=pltpu.CompilerParams(vmem_limit_bytes=56 * 2**20),
            cost_estimate=pl.CostEstimate(flops=hops * 2**31, bytes_accessed=moved, transcendentals=0),
        )(*operands)

    return call


def on_device(object_slices, positions, intensities, probe, propagator):
    measured, offsets = intensities[0, 0], positions[0, 0]
    count, width = measured.shape[0], measured.shape[-1]
    layers, tall, broad = object_slices.shape[1:]
    near = layers // 2
    rest = layers - near
    tables = jnp.asarray(half_tables(width))
    phase = jnp.stack([jnp.cos(propagator), jnp.sin(propagator)])
    ordered, phases = called(entry_kernel, [like(measured), like(phase)], [], 0)(measured, phase, tables)
    ahead = gathered(object_slices[:, :near])
    behind = gathered(object_slices[:, near:])

    def wide_sums(depth):
        return (2, depth, broad // 128 + 1, tall + 2 * HALO, 128)

    def fields(*lead):
        return (count, *lead, 2, width, width)

    def f32(shape):
        return jax.ShapeDtypeStruct(shape, jnp.float32)

    waves, windows = called(
        first_kernel, [f32(fields(near + 1)), f32(fields(near))], [wide_sums(near)], 2 * near, 1
    )(offsets, *ahead, probe, phases, tables)
    *late, slab_back = called(
        turn_kernel,
        [like(v) for v in behind] + [f32(fields())],
        [wide_sums(rest), wide_sums(rest), fields(rest), fields(rest), fields()],
        4 * rest,
        1,
    )(offsets, *behind, waves, ordered, phases, tables)
    early = called(
        last_kernel, [like(v) for v in ahead], [wide_sums(near), fields()], 2 * near, 1
    )(offsets, waves, windows, slab_back, phases, tables)
    late = folded(*late)
    early = folded(*early)
    outs = [like(object_slices), like(object_slices)]
    return tuple(called(final_kernel, outs, [], 0)(*early, *late, object_slices))


def solution(mesh):
    return jax.shard_map(
        on_device,
        mesh=mesh,
        in_specs=(
            P(None, None, "row", "col"),
            P("row", "col", None, None),
            P("row", "col", None, None, None),
            P(),
            P(),
        ),
        out_specs=(P(None, None, "row", "col"), P(None, None, "row", "col")),
        check_vma=False,
    )
```

```python
import jax
import jax.numpy as jnp
import numpy as np
from jax import lax
from jax.experimental import pallas as pl
from jax.experimental.pallas import tpu as pltpu
from jax.sharding import PartitionSpec as P

HALO = 64


descent_rate = 0.5


def passed_along(block, axis, distance):
    devices = range(lax.axis_size(axis))
    route = [((i - distance) % len(devices), i) for i in devices]
    return lax.ppermute(block, axis, route)


def split(value):
    high = value.astype(jnp.bfloat16)
    low = (value - high.astype(jnp.float32)).astype(jnp.bfloat16)
    return high, low


def half_tables(width):
    half = width // 2
    place = np.arange(half)
    found = []
    for odd in (0, 1):
        angle = 2.0 * np.pi * (np.outer(2 * place + odd, place) % width) / width
        re = np.cos(angle) / np.sqrt(width)
        im = -np.sin(angle) / np.sqrt(width)
        found.append(np.block([[re, -im], [im, re]]).astype(np.float32))
    even, odd = found
    order = np.eye(width, dtype=np.float32)[np.concatenate([2 * place, 2 * place + 1])]
    six = np.stack([even, odd, even.T, odd.T, order, order.T])
    high = six.astype(jnp.bfloat16)
    low = (six - high.astype(np.float32)).astype(jnp.bfloat16)
    return np.stack([high, low])


def dot_left(pair, value):
    high, low = split(value)
    matrix = jnp.concatenate([pair[0], pair[0], pair[1]], 1)
    return jnp.dot(matrix, jnp.concatenate([high, low, high], 0), preferred_element_type=jnp.float32)


def dot_right(value, pair):
    high, low = split(value)
    matrix = jnp.concatenate([pair[0], pair[0], pair[1]], 0)
    return jnp.dot(jnp.concatenate([high, low, high], 1), matrix, preferred_element_type=jnp.float32)


def cut(value, dim):
    half = value.shape[dim] // 2
    return (lax.slice_in_dim(value, 0, half, axis=dim), lax.slice_in_dim(value, half, 2 * half, axis=dim))


def joined(first, second, dim):
    return jnp.concatenate([first, second], dim)


def forward_axis(re, im, dim, dot, even_matrix, odd_matrix):
    r0, r1 = cut(re, dim)
    i0, i1 = cut(im, dim)
    even_re, even_im = cut(dot(joined(r0 + r1, i0 + i1, dim), even_matrix), dim)
    odd_re, odd_im = cut(dot(joined(r0 - r1, i0 - i1, dim), odd_matrix), dim)
    return joined(even_re, odd_re, dim), joined(even_im, odd_im, dim)


def inverse_axis(re, im, dim, dot, even_matrix, odd_matrix):
    r0, r1 = cut(re, dim)
    i0, i1 = cut(im, dim)
    p_re, p_im = cut(dot(joined(r0, i0, dim), even_matrix), dim)
    q_re, q_im = cut(dot(joined(r1, i1, dim), odd_matrix), dim)
    return joined(p_re + q_re, p_re - q_re, dim), joined(p_im + q_im, p_im - q_im, dim)


def left_dot(value, pair):
    return dot_left(pair, value)


def forward(re, im, pairs):
    re, im = forward_axis(re, im, 0, left_dot, pairs(0), pairs(1))
    return forward_axis(re, im, 1, dot_right, pairs(2), pairs(3))


def inverse(re, im, pairs):
    re, im = inverse_axis(re, im, 1, dot_right, pairs(0), pairs(1))
    return inverse_axis(re, im, 0, left_dot, pairs(2), pairs(3))


def by_parity(value, pairs):
    return dot_right(dot_left(pairs(4), value), pairs(5))


def complex_product(left_re, left_im, right_re, right_im):
    return (left_re * right_re - left_im * right_im, left_re * right_im + left_im * right_re)


def slid(whole, shift, axis, span):
    turned = pltpu.roll(whole, lax.rem(span - shift, span), axis)
    kept = lax.broadcasted_iota(jnp.int32, whole[:-1].shape, axis) < span - shift
    return jnp.where(kept, turned[:-1], turned[1:])


def spread(whole, shift, axis, span):
    turned = pltpu.roll(whole, lax.rem(shift, span), axis)
    zero = jnp.zeros_like(turned[:1])
    first = jnp.concatenate([zero, turned], 0)
    other = jnp.concatenate([turned, zero], 0)
    moved = lax.broadcasted_iota(jnp.int32, first.shape, axis) < shift
    return jnp.where(moved, first, other)


def row_place(oy, rows, width):
    base = jnp.minimum(oy - lax.rem(oy, 8), rows - width - 8)
    return pl.ds(pl.multiple_of(base, 8), width + 8), oy - base


def lane_place(ox, lanes=128):
    early = ox < HALO
    return jnp.where(early, 2, 0), jnp.where(early, ox + lanes - HALO, ox - HALO)


def swapped(value):
    return pltpu.roll(value, HALO, value.ndim - 1)


def lower_lanes(value):
    return lax.broadcasted_iota(jnp.int32, value.shape, value.ndim - 1) < HALO


def entry_kernel(measured, phase, tables, ordered, phases):
    def pairs(index):
        return tables[0, index], tables[1, index]

    for c in range(2):
        phases[c] = by_parity(phase[c], pairs)
    for k in range(measured.shape[0]):
        ordered[k] = by_parity(measured[k], pairs)


def step_kernel(
    offsets, core, edges, right, left, right_ends, left_ends, ordered, probe, phases, tables,
    out, out_edges, to_right, to_left, to_right_ends, to_left_ends,
    ext, total, windows, waves,
):
    count = ordered.shape[0]
    width = ordered.shape[-1]
    layers = core.shape[1]
    last = layers - 1
    tall = core.shape[2]
    wide = core.shape[3] // 128
    rounds = wide + 1
    whole = tall + 2 * HALO
    pieces = ((0, HALO, True, 0), (HALO, tall, False, 0), (HALO + tall, HALO, True, HALO))

    def pairs(index):
        return tables[0, index], tables[1, index]

    def gather(layer, carry):
        for start, size, is_edge, at in pieces:
            rows, own = pl.ds(start, size), pl.ds(at, size)
            for c in range(2):
                source = edges if is_edge else core
                for j in range(wide):
                    ext[c, layer, j, rows, :] = source[c, layer, own, pl.ds(j * 128, 128)]
            r = (right_ends if is_edge else right)[layer, own, :]
            l = (left_ends if is_edge else left)[layer, own, :]
            low = lower_lanes(r)
            ext[0, layer, wide, rows, :] = jnp.where(low, r, swapped(l))
            ext[1, layer, wide, rows, :] = jnp.where(low, swapped(r), l)
        return carry

    lax.fori_loop(0, layers, gather, 0)
    total[...] = jnp.zeros_like(total)
    for k in range(count):
        waves[k, 0] = probe[...]

    def cut_layer(k, layer):
        rows, shift = row_place(offsets[k, 0], whole, width)
        first, turn = lane_place(offsets[k, 1])
        for c in range(2):
            blocks = jnp.stack(
                [ext[c, layer, lax.rem(first + j, rounds), rows, :] for j in range(rounds)]
            )
            blocks = slid(blocks, turn, 2, 128)
            for j in range(wide):
                part = blocks[j].reshape((width + 8) // 8, 8, 128)
                windows[k, layer, c, :, j * 128 : j * 128 + 128] = slid(part, shift, 1, 8).reshape(width, 128)

    def leave(k, layer):
        return complex_product(
            waves[k, layer, 0], waves[k, layer, 1], windows[k, layer, 0], windows[k, layer, 1]
        )

    def onward(layer, carry):
        for k in range(count):
            cut_layer(k, layer)
            re, im = forward(*leave(k, layer), pairs)
            re, im = complex_product(re, im, phases[0], phases[1])
            re, im = inverse(re, im, pairs)
            waves[k, layer + 1, 0] = re
            waves[k, layer + 1, 1] = im
        return carry

    lax.fori_loop(0, last, onward, 0)

    def record(k, layer, back_re, back_im):
        wave_re, wave_im = waves[k, layer, 0], waves[k, layer, 1]
        rows, shift = row_place(offsets[k, 0], whole, width)
        first, turn = lane_place(offsets[k, 1])
        terms = (wave_re * back_re + wave_im * back_im, wave_re * back_im - wave_im * back_re)
        for c in range(2):
            blocks = jnp.stack([terms[c][:, j * 128 : j * 128 + 128] for j in range(wide)])
            blocks = spread(blocks, turn, 2, 128)
            for j in range(rounds):
                part = spread(blocks[j].reshape(width // 8, 8, 128), shift, 1, 8)
                total[c, layer, lax.rem(first + j, rounds), rows, :] += part.reshape(width + 8, 128)

    for k in range(count):
        cut_layer(k, last)
        far_re, far_im = forward(*leave(k, last), pairs)
        misfit = far_re * far_re + far_im * far_im - ordered[k]
        back_re, back_im = inverse(misfit * far_re, misfit * far_im, pairs)
        record(k, last, back_re, back_im)
        waves[k, last, 0] = back_re
        waves[k, last, 1] = back_im

    def backward(step, carry):
        layer = last - step
        for k in range(count):
            back_re, back_im = waves[k, layer, 0], waves[k, layer, 1]
            slab_re, slab_im = windows[k, layer, 0], windows[k, layer, 1]
            re, im = complex_product(back_re, back_im, slab_re, -slab_im)
            re, im = forward(re, im, pairs)
            re, im = complex_product(re, im, phases[0], -phases[1])
            re, im = inverse(re, im, pairs)
            record(k, layer - 1, re, im)
            waves[k, layer - 1, 0] = re
            waves[k, layer - 1, 1] = im
        return carry

    lax.fori_loop(0, last, backward, 0)

    def hand_out(layer, carry):
        for start, size, is_edge, at in pieces:
            rows, own = pl.ds(start, size), pl.ds(at, size)
            for c in range(2):
                target = out_edges if is_edge else out
                for j in range(wide):
                    target[c, layer, own, pl.ds(j * 128, 128)] = total[c, layer, j, rows, :]
            re, im = total[0, layer, wide, rows, :], total[1, layer, wide, rows, :]
            low = lower_lanes(re)
            (to_right_ends if is_edge else to_right)[layer, own, :] = jnp.where(low, re, swapped(im))
            (to_left_ends if is_edge else to_left)[layer, own, :] = jnp.where(low, swapped(re), im)
        return carry

    lax.fori_loop(0, layers, hand_out, 0)


def packed(cells):
    wide = cells.shape[-1]
    head = jnp.concatenate([cells[0, ..., :HALO], cells[1, ..., :HALO]], -1)
    tail = jnp.concatenate([cells[0, ..., wide - HALO :], cells[1, ..., wide - HALO :]], -1)
    return head, tail


def like(array):
    return jax.ShapeDtypeStruct(array.shape, array.dtype)


def absorb(parts, cells, from_left, from_right):
    wide = cells.shape[-1]
    l, r = from_left[...], from_right[...]
    low = lower_lanes(l)
    zero = jnp.zeros_like(l)
    added = (
        (jnp.where(low, l, zero), jnp.where(low, zero, swapped(r))),
        (jnp.where(low, swapped(l), zero), jnp.where(low, zero, r)),
    )
    for c in range(2):
        parts[c, :, :, 0:128] = cells[c, :, :, 0:128] + added[c][0]
        for at in range(128, wide - 128, 128):
            parts[c, :, :, at : at + 128] = cells[c, :, :, at : at + 128]
        parts[c, :, :, wide - 128 : wide] = cells[c, :, :, wide - 128 : wide] + added[c][1]


def edges_kernel(edges, from_left, from_right, up, down):
    size = edges.shape[2] // 2
    top, bottom = pl.ds(0, size), pl.ds(size, size)
    absorb(up, edges.at[:, :, top, :], from_left.at[:, top, :], from_right.at[:, top, :])
    absorb(down, edges.at[:, :, bottom, :], from_left.at[:, bottom, :], from_right.at[:, bottom, :])


def final_kernel(cells, from_left, from_right, from_above, from_below, objects, gradient, updated):
    tall = cells.shape[2]
    absorb(gradient, cells, from_left, from_right)
    gradient[:, :, 0:HALO, :] += from_above[...]
    gradient[:, :, tall - HALO : tall, :] += from_below[...]
    updated[...] = objects[...] - descent_rate * gradient[...]


def on_device(object_slices, positions, intensities, probe, propagator):
    measured = intensities[0, 0]
    count, width = measured.shape[0], measured.shape[-1]
    layers, tall, broad = object_slices.shape[1:]
    wide = broad // 128
    tables = jnp.asarray(half_tables(width))
    phase = jnp.stack([jnp.cos(propagator), jnp.sin(propagator)])
    ordered, phases = pl.pallas_call(
        entry_kernel,
        out_shape=[like(measured), like(phase)],
        in_specs=[pl.BlockSpec(memory_space=pltpu.VMEM)] * 3,
        out_specs=[pl.BlockSpec(memory_space=pltpu.VMEM)] * 2,
        cost_estimate=pl.CostEstimate(flops=2**30, bytes_accessed=2**22, transcendentals=0),
    )(measured, phase, tables)
    above = passed_along(object_slices[:, :, tall - HALO :], "row", 1)
    below = passed_along(object_slices[:, :, :HALO], "row", -1)
    head, tail = packed(object_slices)
    right = passed_along(head, "col", -1)
    left = passed_along(tail, "col", 1)
    edges = jnp.concatenate([above, below], 2)
    head, tail = packed(edges)
    right_ends = passed_along(head, "col", -1)
    left_ends = passed_along(tail, "col", 1)
    vmem = pl.BlockSpec(memory_space=pltpu.VMEM)
    limit = pltpu.CompilerParams(vmem_limit_bytes=58 * 2**20)
    cells, edges, to_right, to_left, to_right_ends, to_left_ends = pl.pallas_call(
        step_kernel,
        out_shape=[like(v) for v in (object_slices, edges, right, left, right_ends, left_ends)],
        in_specs=[pl.BlockSpec(memory_space=pltpu.SMEM)] + [vmem] * 10,
        out_specs=[vmem] * 6,
        scratch_shapes=[
            pltpu.VMEM((2, layers, wide + 1, tall + 2 * HALO, 128), jnp.float32),
            pltpu.VMEM((2, layers, wide + 1, tall + 2 * HALO, 128), jnp.float32),
            pltpu.VMEM((count, layers, 2, width, width), jnp.float32),
            pltpu.VMEM((count, layers, 2, width, width), jnp.float32),
        ],
        compiler_params=limit,
    )(
        positions[0, 0], object_slices, edges, right, left, right_ends, left_ends,
        ordered, probe, phases, tables,
    )
    left_ends = passed_along(to_right_ends, "col", 1)
    right_ends = passed_along(to_left_ends, "col", -1)
    left = passed_along(to_right, "col", 1)
    right = passed_along(to_left, "col", -1)
    up, down = pl.pallas_call(
        edges_kernel,
        out_shape=[like(above), like(below)],
        in_specs=[vmem] * 3,
        out_specs=[vmem] * 2,
        compiler_params=limit,
    )(edges, left_ends, right_ends)
    from_above = passed_along(down, "row", 1)
    from_below = passed_along(up, "row", -1)
    plane = pl.BlockSpec((2, 1, tall, broad), lambda layer: (0, layer, 0, 0))
    strip = pl.BlockSpec((1, tall, 128), lambda layer: (layer, 0, 0))
    border = pl.BlockSpec((2, 1, HALO, broad), lambda layer: (0, layer, 0, 0))
    return tuple(
        pl.pallas_call(
            final_kernel,
            grid=(layers,),
            out_shape=[like(cells), like(cells)],
            in_specs=[plane, strip, strip, border, border, plane],
            out_specs=[plane, plane],
            compiler_params=limit,
        )(cells, left, right, from_above, from_below, object_slices)
    )


def solution(mesh):
    return jax.shard_map(
        on_device,
        mesh=mesh,
        in_specs=(
            P(None, None, "row", "col"),
            P("row", "col", None, None),
            P("row", "col", None, None, None),
            P(),
            P(),
        ),
        out_specs=(P(None, None, "row", "col"), P(None, None, "row", "col")),
        check_vma=False,
    )
```

```python
import jax
import jax.numpy as jnp
import numpy as np
from jax import lax
from jax.experimental import pallas as pl
from jax.experimental.pallas import tpu as pltpu
from jax.sharding import PartitionSpec as P

HALO = 64


descent_rate = 0.5


def passed_along(block, axis, distance):
    devices = range(lax.axis_size(axis))
    route = [((i - distance) % len(devices), i) for i in devices]
    return lax.ppermute(block, axis, route)


def split(value):
    high = value.astype(jnp.bfloat16)
    low = (value - high.astype(jnp.float32)).astype(jnp.bfloat16)
    return high, low


def half_tables(width):
    half = width // 2
    place = np.arange(half)
    found = []
    for odd in (0, 1):
        angle = 2.0 * np.pi * (np.outer(2 * place + odd, place) % width) / width
        re = np.cos(angle) / np.sqrt(width)
        im = -np.sin(angle) / np.sqrt(width)
        found.append(np.block([[re, -im], [im, re]]).astype(np.float32))
    even, odd = found
    order = np.eye(width, dtype=np.float32)[np.concatenate([2 * place, 2 * place + 1])]
    six = np.stack([even, odd, even.T, odd.T, order, order.T])
    high = six.astype(jnp.bfloat16)
    low = (six - high.astype(np.float32)).astype(jnp.bfloat16)
    return np.stack([high, low])


def dot_left(pair, value):
    high, low = split(value)
    matrix = jnp.concatenate([pair[0], pair[0], pair[1]], 1)
    return jnp.dot(matrix, jnp.concatenate([high, low, high], 0), preferred_element_type=jnp.float32)


def dot_right(value, pair):
    high, low = split(value)
    matrix = jnp.concatenate([pair[0], pair[0], pair[1]], 0)
    return jnp.dot(jnp.concatenate([high, low, high], 1), matrix, preferred_element_type=jnp.float32)


def cut(value, dim):
    half = value.shape[dim] // 2
    return (lax.slice_in_dim(value, 0, half, axis=dim), lax.slice_in_dim(value, half, 2 * half, axis=dim))


def joined(first, second, dim):
    return jnp.concatenate([first, second], dim)


def forward_axis(re, im, dim, dot, even_matrix, odd_matrix):
    r0, r1 = cut(re, dim)
    i0, i1 = cut(im, dim)
    even_re, even_im = cut(dot(joined(r0 + r1, i0 + i1, dim), even_matrix), dim)
    odd_re, odd_im = cut(dot(joined(r0 - r1, i0 - i1, dim), odd_matrix), dim)
    return joined(even_re, odd_re, dim), joined(even_im, odd_im, dim)


def inverse_axis(re, im, dim, dot, even_matrix, odd_matrix):
    r0, r1 = cut(re, dim)
    i0, i1 = cut(im, dim)
    p_re, p_im = cut(dot(joined(r0, i0, dim), even_matrix), dim)
    q_re, q_im = cut(dot(joined(r1, i1, dim), odd_matrix), dim)
    return joined(p_re + q_re, p_re - q_re, dim), joined(p_im + q_im, p_im - q_im, dim)


def left_dot(value, pair):
    return dot_left(pair, value)


def turned_over(value, width, source, target):
    parts = [lax.slice_in_dim(value, at, at + width, axis=source) for at in range(0, value.shape[source], width)]
    return jnp.concatenate(parts, target)


def forward(re, im, pairs):
    width = re.shape[0]
    re, im = forward_axis(re, im, 0, left_dot, pairs(0), pairs(1))
    re, im = (turned_over(v, width, 1, 0) for v in (re, im))
    return forward_axis(re, im, 1, dot_right, pairs(2), pairs(3))


def inverse(re, im, pairs):
    width = re.shape[1]
    re, im = inverse_axis(re, im, 1, dot_right, pairs(0), pairs(1))
    re, im = (turned_over(v, width, 0, 1) for v in (re, im))
    return inverse_axis(re, im, 0, left_dot, pairs(2), pairs(3))


def hop(fields, phase_re, phase_im, pairs):
    width = fields[0][0].shape[0]
    re, im = forward(*(jnp.concatenate([f[c] for f in fields], 1) for c in range(2)), pairs)
    re, im = complex_product(re, im, *(jnp.concatenate([p] * len(fields), 0) for p in (phase_re, phase_im)))
    re, im = inverse(re, im, pairs)
    spans = [slice(at, at + width) for at in range(0, re.shape[1], width)]
    return [(re[:, span], im[:, span]) for span in spans]


def by_parity(value, pairs):
    return dot_right(dot_left(pairs(4), value), pairs(5))


def complex_product(left_re, left_im, right_re, right_im):
    return (left_re * right_re - left_im * right_im, left_re * right_im + left_im * right_re)


def slid(whole, shift, axis, span):
    turned = pltpu.roll(whole, lax.rem(span - shift, span), axis)
    kept = lax.broadcasted_iota(jnp.int32, whole[:-1].shape, axis) < span - shift
    return jnp.where(kept, turned[:-1], turned[1:])


def spread(whole, shift, axis, span):
    turned = pltpu.roll(whole, lax.rem(shift, span), axis)
    zero = jnp.zeros_like(turned[:1])
    first = jnp.concatenate([zero, turned], 0)
    other = jnp.concatenate([turned, zero], 0)
    moved = lax.broadcasted_iota(jnp.int32, first.shape, axis) < shift
    return jnp.where(moved, first, other)


def row_place(oy, rows, width):
    base = jnp.minimum(oy - lax.rem(oy, 8), rows - width - 8)
    return pl.ds(pl.multiple_of(base, 8), width + 8), oy - base


def lane_place(ox, lanes=128):
    early = ox < HALO
    return jnp.where(early, 2, 0), jnp.where(early, ox + lanes - HALO, ox - HALO)


def swapped(value):
    return pltpu.roll(value, HALO, value.ndim - 1)


def lower_lanes(value):
    return lax.broadcasted_iota(jnp.int32, value.shape, value.ndim - 1) < HALO


def entry_kernel(measured, phase, tables, ordered, phases):
    def pairs(index):
        return tables[0, index], tables[1, index]

    for c in range(2):
        phases[c] = by_parity(phase[c], pairs)
    for k in range(measured.shape[0]):
        ordered[k] = by_parity(measured[k], pairs)


def step_kernel(
    offsets, core, edges, right, left, right_ends, left_ends, ordered, probe, phases, tables,
    out, out_edges, to_right, to_left, to_right_ends, to_left_ends,
    ext, total, windows, waves,
):
    count = ordered.shape[0]
    width = ordered.shape[-1]
    layers = core.shape[1]
    last = layers - 1
    tall = core.shape[2]
    wide = core.shape[3] // 128
    rounds = wide + 1
    whole = tall + 2 * HALO
    pieces = ((0, HALO, True, 0), (HALO, tall, False, 0), (HALO + tall, HALO, True, HALO))

    def pairs(index):
        return tables[0, index], tables[1, index]

    def gather(layer, carry):
        for start, size, is_edge, at in pieces:
            rows, own = pl.ds(start, size), pl.ds(at, size)
            for c in range(2):
                source = edges if is_edge else core
                for j in range(wide):
                    ext[c, layer, j, rows, :] = source[c, layer, own, pl.ds(j * 128, 128)]
            r = (right_ends if is_edge else right)[layer, own, :]
            l = (left_ends if is_edge else left)[layer, own, :]
            low = lower_lanes(r)
            ext[0, layer, wide, rows, :] = jnp.where(low, r, swapped(l))
            ext[1, layer, wide, rows, :] = jnp.where(low, swapped(r), l)
        return carry

    lax.fori_loop(0, layers, gather, 0)
    total[...] = jnp.zeros_like(total)
    for k in range(count):
        waves[k, 0] = probe[...]

    def cut_layer(k, layer):
        rows, shift = row_place(offsets[k, 0], whole, width)
        first, turn = lane_place(offsets[k, 1])
        for c in range(2):
            blocks = jnp.stack(
                [ext[c, layer, lax.rem(first + j, rounds), rows, :] for j in range(rounds)]
            )
            blocks = slid(blocks, turn, 2, 128)
            for j in range(wide):
                part = blocks[j].reshape((width + 8) // 8, 8, 128)
                windows[k, layer, c, :, j * 128 : j * 128 + 128] = slid(part, shift, 1, 8).reshape(width, 128)

    def leave(k, layer):
        return complex_product(
            waves[k, layer, 0], waves[k, layer, 1], windows[k, layer, 0], windows[k, layer, 1]
        )

    def onward(layer, carry):
        for k in range(count):
            cut_layer(k, layer)
        fields = [leave(k, layer) for k in range(count)]
        for k, (re, im) in enumerate(hop(fields, phases[0], phases[1], pairs)):
            waves[k, layer + 1, 0] = re
            waves[k, layer + 1, 1] = im
        return carry

    lax.fori_loop(0, last, onward, 0)

    def record(k, layer, back_re, back_im):
        wave_re, wave_im = waves[k, layer, 0], waves[k, layer, 1]
        rows, shift = row_place(offsets[k, 0], whole, width)
        first, turn = lane_place(offsets[k, 1])
        terms = (wave_re * back_re + wave_im * back_im, wave_re * back_im - wave_im * back_re)
        for c in range(2):
            blocks = jnp.stack([terms[c][:, j * 128 : j * 128 + 128] for j in range(wide)])
            blocks = spread(blocks, turn, 2, 128)
            for j in range(rounds):
                part = spread(blocks[j].reshape(width // 8, 8, 128), shift, 1, 8)
                total[c, layer, lax.rem(first + j, rounds), rows, :] += part.reshape(width + 8, 128)

    for k in range(count):
        cut_layer(k, last)
        far_re, far_im = forward(*leave(k, last), pairs)
        misfit = far_re * far_re + far_im * far_im - ordered[k]
        back_re, back_im = inverse(misfit * far_re, misfit * far_im, pairs)
        record(k, last, back_re, back_im)
        waves[k, last, 0] = back_re
        waves[k, last, 1] = back_im

    def backward(step, carry):
        layer = last - step
        fields = []
        for k in range(count):
            back_re, back_im = waves[k, layer, 0], waves[k, layer, 1]
            slab_re, slab_im = windows[k, layer, 0], windows[k, layer, 1]
            fields.append(complex_product(back_re, back_im, slab_re, -slab_im))
        for k, (re, im) in enumerate(hop(fields, phases[0], -phases[1], pairs)):
            record(k, layer - 1, re, im)
            waves[k, layer - 1, 0] = re
            waves[k, layer - 1, 1] = im
        return carry

    lax.fori_loop(0, last, backward, 0)

    def hand_out(layer, carry):
        for start, size, is_edge, at in pieces:
            rows, own = pl.ds(start, size), pl.ds(at, size)
            for c in range(2):
                target = out_edges if is_edge else out
                for j in range(wide):
                    target[c, layer, own, pl.ds(j * 128, 128)] = total[c, layer, j, rows, :]
            re, im = total[0, layer, wide, rows, :], total[1, layer, wide, rows, :]
            low = lower_lanes(re)
            (to_right_ends if is_edge else to_right)[layer, own, :] = jnp.where(low, re, swapped(im))
            (to_left_ends if is_edge else to_left)[layer, own, :] = jnp.where(low, swapped(re), im)
        return carry

    lax.fori_loop(0, layers, hand_out, 0)


def packed(cells):
    wide = cells.shape[-1]
    head = jnp.concatenate([cells[0, ..., :HALO], cells[1, ..., :HALO]], -1)
    tail = jnp.concatenate([cells[0, ..., wide - HALO :], cells[1, ..., wide - HALO :]], -1)
    return head, tail


def like(array):
    return jax.ShapeDtypeStruct(array.shape, array.dtype)


def absorb(parts, cells, from_left, from_right):
    wide = cells.shape[-1]
    l, r = from_left[...], from_right[...]
    low = lower_lanes(l)
    zero = jnp.zeros_like(l)
    added = (
        (jnp.where(low, l, zero), jnp.where(low, zero, swapped(r))),
        (jnp.where(low, swapped(l), zero), jnp.where(low, zero, r)),
    )
    for c in range(2):
        parts[c, :, :, 0:128] = cells[c, :, :, 0:128] + added[c][0]
        for at in range(128, wide - 128, 128):
            parts[c, :, :, at : at + 128] = cells[c, :, :, at : at + 128]
        parts[c, :, :, wide - 128 : wide] = cells[c, :, :, wide - 128 : wide] + added[c][1]


def edges_kernel(edges, from_left, from_right, up, down):
    size = edges.shape[2] // 2
    top, bottom = pl.ds(0, size), pl.ds(size, size)
    absorb(up, edges.at[:, :, top, :], from_left.at[:, top, :], from_right.at[:, top, :])
    absorb(down, edges.at[:, :, bottom, :], from_left.at[:, bottom, :], from_right.at[:, bottom, :])


def final_kernel(cells, from_left, from_right, from_above, from_below, objects, gradient, updated):
    tall = cells.shape[2]
    absorb(gradient, cells, from_left, from_right)
    gradient[:, :, 0:HALO, :] += from_above[...]
    gradient[:, :, tall - HALO : tall, :] += from_below[...]
    updated[...] = objects[...] - descent_rate * gradient[...]


def on_device(object_slices, positions, intensities, probe, propagator):
    measured = intensities[0, 0]
    count, width = measured.shape[0], measured.shape[-1]
    layers, tall, broad = object_slices.shape[1:]
    wide = broad // 128
    tables = jnp.asarray(half_tables(width))
    phase = jnp.stack([jnp.cos(propagator), jnp.sin(propagator)])
    ordered, phases = pl.pallas_call(
        entry_kernel,
        out_shape=[like(measured), like(phase)],
        in_specs=[pl.BlockSpec(memory_space=pltpu.VMEM)] * 3,
        out_specs=[pl.BlockSpec(memory_space=pltpu.VMEM)] * 2,
        cost_estimate=pl.CostEstimate(flops=2**30, bytes_accessed=2**22, transcendentals=0),
    )(measured, phase, tables)
    above = passed_along(object_slices[:, :, tall - HALO :], "row", 1)
    below = passed_along(object_slices[:, :, :HALO], "row", -1)
    head, tail = packed(object_slices)
    right = passed_along(head, "col", -1)
    left = passed_along(tail, "col", 1)
    edges = jnp.concatenate([above, below], 2)
    head, tail = packed(edges)
    right_ends = passed_along(head, "col", -1)
    left_ends = passed_along(tail, "col", 1)
    vmem = pl.BlockSpec(memory_space=pltpu.VMEM)
    limit = pltpu.CompilerParams(vmem_limit_bytes=58 * 2**20)
    cells, edges, to_right, to_left, to_right_ends, to_left_ends = pl.pallas_call(
        step_kernel,
        out_shape=[like(v) for v in (object_slices, edges, right, left, right_ends, left_ends)],
        in_specs=[pl.BlockSpec(memory_space=pltpu.SMEM)] + [vmem] * 10,
        out_specs=[vmem] * 6,
        scratch_shapes=[
            pltpu.VMEM((2, layers, wide + 1, tall + 2 * HALO, 128), jnp.float32),
            pltpu.VMEM((2, layers, wide + 1, tall + 2 * HALO, 128), jnp.float32),
            pltpu.VMEM((count, layers, 2, width, width), jnp.float32),
            pltpu.VMEM((count, layers, 2, width, width), jnp.float32),
        ],
        compiler_params=limit,
    )(
        positions[0, 0], object_slices, edges, right, left, right_ends, left_ends,
        ordered, probe, phases, tables,
    )
    left_ends = passed_along(to_right_ends, "col", 1)
    right_ends = passed_along(to_left_ends, "col", -1)
    left = passed_along(to_right, "col", 1)
    right = passed_along(to_left, "col", -1)
    up, down = pl.pallas_call(
        edges_kernel,
        out_shape=[like(above), like(below)],
        in_specs=[vmem] * 3,
        out_specs=[vmem] * 2,
        compiler_params=limit,
    )(edges, left_ends, right_ends)
    from_above = passed_along(down, "row", 1)
    from_below = passed_along(up, "row", -1)
    plane = pl.BlockSpec((2, 1, tall, broad), lambda layer: (0, layer, 0, 0))
    strip = pl.BlockSpec((1, tall, 128), lambda layer: (layer, 0, 0))
    border = pl.BlockSpec((2, 1, HALO, broad), lambda layer: (0, layer, 0, 0))
    return tuple(
        pl.pallas_call(
            final_kernel,
            grid=(layers,),
            out_shape=[like(cells), like(cells)],
            in_specs=[plane, strip, strip, border, border, plane],
            out_specs=[plane, plane],
            compiler_params=limit,
        )(cells, left, right, from_above, from_below, object_slices)
    )


def solution(mesh):
    return jax.shard_map(
        on_device,
        mesh=mesh,
        in_specs=(
            P(None, None, "row", "col"),
            P("row", "col", None, None),
            P("row", "col", None, None, None),
            P(),
            P(),
        ),
        out_specs=(P(None, None, "row", "col"), P(None, None, "row", "col")),
        check_vma=False,
    )
```
